32 devices in a mesh: docs: 8 (over z, x), topics: 4 (over y, core).
Axes of the slice: x: 2, y: 2, z: 4, core: 2. Of those that a mesh axis runs over, the one named last changes fastest.
Arguments:
- log_beta: bfloat16 [262144, 2048], P('docs', 'topics'), may hold values from -250 to -4
- gamma_init: float32 [128, 2048], P('docs', 'topics'), may hold values from 0.05 to 5
- topic_prior: float32 [2048], P('topics'), may hold values from 0.02 to 0.5
- word_block: int32 [128, 256, 1], P('docs'), may hold values from 0 to 7; in each aligned block of 4096 rows (0 to 4095, 4096 to 8191, ..., all dimensions but the last counted through in order) at most 1024 rows name the same one
- word_row: int32 [128, 256], P('docs'), may hold values from 0 to 32767
- counts: int32 [128, 256], P('docs'), may hold values from 0 to 2
Outputs:
- doc_gamma: float32 [128, 2048], P('docs', 'topics')
- sstats: float32 [262144, 2048], P('docs', 'topics')
The draws below stay inside these ranges and needn't reach their ends.
Inputs may be any that keep to these rules, and one draw needn't show every extreme that they name: `word_block`: among the token slots of one device's 16 documents, at most 1024 name the same vocabulary block, and some block is named by exactly 1024 of them on some device. `counts`: A count of 0 marks an empty slot.
All inputs are finite; a program needn't handle non-finite values.
Results may differ from the reference program's by a relative error of at most 0.0003.
Values may be sent and summed in bfloat16 or wider, within the bound.
A program may use at most 192 MiB of HBM per device.

```python
import math
import jax
import jax.numpy as jnp
import numpy as np
from jax import lax

K = 2048
VOCAB = 262144
LEN = 256
ITERS = 3
DOC_DEV = 16
DOCS = 128
VOC_DEV = 32768
CAP = 1024
N_DOCS = 8


def draw_log_beta(key, part):
    values = jax.random.uniform(key, (VOCAB, K), jnp.float32, -14.0, -4.0)
    return values.astype(jnp.bfloat16)


def place_ends(result, key, least, largest):
    spot = [jax.random.randint(jax.random.fold_in(key, axis), (), 0, length) for axis, length in enumerate(result.shape)]
    widest = result.shape.index(max(result.shape))
    beside = spot[:widest] + [(spot[widest] + 1) % result.shape[widest]] + spot[widest + 1:]
    return result.at[tuple(spot)].set(least).at[tuple(beside)].set(largest)


def levels(key, extent, cuts, low, top_value):
    level, own = 1.0, jax.random.fold_in(key, 6)
    for dim, parts in cuts:
        heights = jnp.exp(jax.random.uniform(jax.random.fold_in(own, dim), (parts,), jnp.float32, low / len(cuts), top_value / len(cuts)))
        level = level * jnp.repeat(heights, extent[dim] // parts).reshape([-1 if axis == dim else 1 for axis in range(len(extent))])
    return level


def assign_block(rng, own, number, rows, count, top, bound, slope):
    order = jax.random.permutation(rng, count)
    packed, common = load_shares(count, rows * top, bound, slope, True), load_shares(count, rows * top, bound, slope, False)
    places = jnp.arange(count)

    def named(lengths, offset_by):
        used = int((lengths > 0).sum())
        fixed = max(1, used // 4)
        shifted = fixed + (places - fixed + offset_by * (used - fixed)) % max(1, count - fixed)
        return jnp.zeros((count,), jnp.int32).at[order[jnp.where(places < fixed, places, shifted)]].set(jnp.asarray(lengths, jnp.int32))

    lengths = jnp.where(number % 4 == 0, named(packed, number // 4), named(common, number - number // 4 - 1))
    mixed = jax.random.permutation(jax.random.fold_in(own, 3), count)
    source_of, receiver = mixed[0:count // 2 * 2:2], mixed[1:count // 2 * 2:2]
    room = jnp.minimum(lengths[source_of] - 1, bound - lengths[receiver]) // 2
    room = jnp.where((source_of == order[0]) | (receiver == order[0]) | (lengths[receiver] == 0), 0, jnp.maximum(room, 0))
    shifted = jax.random.randint(jax.random.fold_in(own, 4), (count // 2,), 0, 1 << 20) % (room + 1)
    lengths = lengths.at[source_of].add(-shifted).at[receiver].add(shifted)
    labels = jnp.searchsorted(jnp.cumsum(lengths), jnp.arange(rows * top), side="right").astype(jnp.int32)
    listing = labels.reshape(top, rows).T
    listing = listing[jax.random.permutation(jax.random.fold_in(own, 1), rows)]
    offset_by = jax.random.randint(jax.random.fold_in(own, 2), (rows, 1), 0, top)
    return jnp.take_along_axis(listing, (jnp.arange(top)[None, :] + offset_by) % top, axis=1)


def load_shares(number_of, total, bound, skew, full):
    weights = [(1 << 20) // math.isqrt(standing ** skew) + 1 for standing in range(1, number_of + 1)]
    largest = bound if full else min(bound, max(-(-total // number_of), total * weights[0] // sum(weights)))
    least = 1 if total - largest >= number_of - 1 else 0
    given, rest = [largest] + [least] * (number_of - 1), total - largest - least * (number_of - 1)
    while rest > 0:
        free = [i for i in range(1, number_of) if given[i] < largest] or [i for i in range(1, number_of) if given[i] < bound]
        pool, budget = sum([weights[i] for i in free]), rest
        for i in free:
            addition = min(bound - given[i], max(1, budget * weights[i] // pool), rest)
            given[i] = given[i] + addition
            rest = rest - addition
    return np.array(given)


def setup_inputs(seed: int = 0) -> dict:
    splits = jax.random.split(jax.random.key(seed), 7)
    log_beta = draw_log_beta(jax.random.fold_in(splits[6], 71), 0)
    gamma_init = jnp.clip(jnp.exp(math.log(5.0) - 4.6051702 * jax.random.uniform(splits[1], (DOCS, K), jnp.float32) ** levels(splits[1], (DOCS, K), ((0, 8), (1, 4)), -0.2, 0.2)), 0.05, 5.0)
    topic_prior = jnp.clip(jnp.exp(math.log(0.5) - 3.218876 * jax.random.uniform(splits[2], (K,), jnp.float32) ** levels(splits[2], (K,), ((0, 4),), -0.2, 0.2)), 0.02, 0.5)
    word_block_keys = jax.random.split(jax.random.fold_in(splits[3], 1), DOCS * LEN // (DOC_DEV * LEN))
    word_block_turns = jax.random.permutation(jax.random.fold_in(splits[3], 3), DOCS * LEN // (DOC_DEV * LEN))
    word_block = jax.vmap(lambda own, number: assign_block(jax.random.fold_in(splits[3], 2), own, number, DOC_DEV * LEN, N_DOCS, 1, CAP, 1))(word_block_keys, word_block_turns).reshape((DOCS, LEN, 1))
    word_row = place_ends(jax.random.randint(splits[4], (DOCS, LEN), 0, VOC_DEV), jax.random.fold_in(splits[4], 1), 0, VOC_DEV - 1).astype(jnp.int32)
    counts = place_ends(jax.random.randint(splits[5], (DOCS, LEN), 0, 3), jax.random.fold_in(splits[5], 1), 0, 2).astype(jnp.int32)
    return {"log_beta": log_beta, "gamma_init": gamma_init, "topic_prior": topic_prior, "word_block": word_block, "word_row": word_row, "counts": counts}


def expect_log(doc_gamma):
    return lax.digamma(doc_gamma)


def token_weights(log_theta, beta_rows):
    scores = log_theta[:, None, :] + beta_rows.astype(jnp.float32)
    row_max = jnp.max(scores, axis=2)
    exp_mass = jnp.sum(jnp.exp(scores - row_max[:, :, None]), axis=2)
    log_norm = row_max + jnp.log(exp_mass)
    return jnp.exp(scores - log_norm[:, :, None])


def reference(log_beta, gamma_init, topic_prior, word_block, word_row, counts):
    word_ids = word_block[:, :, 0] * VOC_DEV + word_row
    word_sets = word_ids.reshape(N_DOCS, DOC_DEV, LEN)
    count_sets = counts.astype(jnp.float32).reshape(N_DOCS, DOC_DEV, LEN)
    doc_gamma = gamma_init
    for sweep_index in range(ITERS):
        log_theta = expect_log(doc_gamma).reshape(N_DOCS, DOC_DEV, K)

        def renew_block(pieces):
            theta_part, word_part, count_part = pieces
            topic_share = token_weights(theta_part, log_beta[word_part])
            return topic_prior[None, :] + jnp.einsum("dn,dnk->dk", count_part, topic_share, precision=lax.Precision.HIGHEST)

        doc_gamma = lax.map(renew_block, (log_theta, word_sets, count_sets)).reshape(DOCS, K)
    final_theta = expect_log(doc_gamma).reshape(N_DOCS, DOC_DEV, K)

    def accumulate(doc_block, sstats):
        word_part = word_sets[doc_block]
        topic_share = token_weights(final_theta[doc_block], log_beta[word_part])
        contrib = count_sets[doc_block][:, :, None] * topic_share
        return sstats.at[word_part.reshape(-1)].add(contrib.reshape(-1, K))

    sstats = lax.fori_loop(0, N_DOCS, accumulate, jnp.zeros((VOCAB, K), jnp.float32))
    return doc_gamma, sstats
```

```python
import functools

import jax
import jax.numpy as jnp
from jax import lax
from jax.experimental import pallas as pl
from jax.experimental.pallas import tpu as pltpu
from jax.sharding import PartitionSpec as P

ITERS = 3
CHUNKS = 8
GROUP = 16
UNROLL = 4
VMEM_LIMIT = 60 * 1024 * 1024


def gather_kernel(row_ref, bound_ref, beta_ref, out_ref, held, sems):
    total, cols = held.shape
    step = total // CHUNKS
    slots = out_ref.shape[0]

    def copy(c):
        return pltpu.make_async_copy(
            beta_ref.at[pl.ds(c * step, step)], held.at[pl.ds(c * step, step)], sems.at[c]
        )

    for c in range(CHUNKS):
        copy(c).start()
    lane_row = lax.broadcasted_iota(jnp.int32, (8, cols), 0)

    def group(g, carry):
        base = pl.multiple_of(g * GROUP, GROUP)
        halves = []
        for half in range(GROUP // 8):
            kept = jnp.zeros((8, cols), jnp.float32)
            for j in range(8):
                row = row_ref[base + half * 8 + j]
                tile = held[pl.ds(pl.multiple_of((row >> 4) << 4, 16), 16), :].astype(jnp.float32)
                eight = jnp.where((row & 8) != 0, tile[8:], tile[:8])
                kept = jnp.where(lane_row == j, pltpu.roll(eight, (j - row) & 7, 0), kept)
            halves.append(kept)
        out_ref[pl.ds(base, GROUP), :] = jnp.concatenate(halves, axis=0).astype(out_ref.dtype)
        return carry

    for c in range(CHUNKS):
        copy(c).wait()
        lax.fori_loop(bound_ref[c], bound_ref[c + 1], group, 0)

    def blank(g, carry):
        out_ref[pl.ds(pl.multiple_of(g * GROUP, GROUP), GROUP), :] = jnp.zeros(
            (GROUP, cols), out_ref.dtype
        )
        return carry

    lax.fori_loop(bound_ref[CHUNKS], slots // GROUP, blank, 0)


def gather_rows(log_beta, rows, bounds):
    slots, (total, cols) = rows.shape[0], log_beta.shape
    return pl.pallas_call(
        gather_kernel,
        out_shape=jax.ShapeDtypeStruct((slots, cols), log_beta.dtype),
        in_specs=[
            pl.BlockSpec(memory_space=pltpu.SMEM),
            pl.BlockSpec(memory_space=pltpu.SMEM),
            pl.BlockSpec(memory_space=pl.ANY),
        ],
        out_specs=pl.BlockSpec(memory_space=pltpu.VMEM),
        scratch_shapes=[
            pltpu.VMEM((total, cols), log_beta.dtype),
            pltpu.SemaphoreType.DMA((CHUNKS,)),
        ],
        compiler_params=pltpu.CompilerParams(vmem_limit_bytes=VMEM_LIMIT),
    )(rows, bounds, log_beta)


def stats_kernel(row_ref, doc_ref, weight_ref, bound_ref, theta_ref, mass_ref, out_ref):
    block = pl.program_id(0)
    height, cols = out_ref.shape
    out_ref[...] = jnp.zeros_like(out_ref)
    begin, end = bound_ref[block], bound_ref[block + 1]

    def step(i, carry):
        last, total = carry
        for j in range(UNROLL):
            place = begin + i * UNROLL + j
            slot = jnp.minimum(place, end - 1)
            weight = jnp.where(place < end, weight_ref[slot], 0.0)
            row = row_ref[slot]
            term = weight * (theta_ref[pl.ds(doc_ref[slot], 1), :] * mass_ref[pl.ds(slot, 1), :])
            total = jnp.where(row == last, total, 0.0) + term
            out_ref[pl.ds(row - block * height, 1), :] = total
            last = row
        return last, total

    lax.fori_loop(
        0,
        (end - begin + UNROLL - 1) // UNROLL,
        step,
        (jnp.int32(-1), jnp.zeros((1, cols), jnp.float32)),
    )


def write_stats(rows, docs, weights, bounds, theta_all, mass, total, height):
    cols = mass.shape[1]
    smem = pl.BlockSpec(memory_space=pltpu.SMEM)
    vmem = pl.BlockSpec(memory_space=pltpu.VMEM)
    return pl.pallas_call(
        stats_kernel,
        grid=(total // height,),
        out_shape=jax.ShapeDtypeStruct((total, cols), jnp.float32),
        in_specs=[smem, smem, smem, smem, vmem, vmem],
        out_specs=pl.BlockSpec((height, cols), lambda b: (b, 0)),
        compiler_params=pltpu.CompilerParams(vmem_limit_bytes=VMEM_LIMIT),
    )(rows, docs, weights, bounds, theta_all, mass)


def swap(blocks):
    return lax.all_to_all(blocks, "docs", split_axis=0, concat_axis=0, tiled=True)


def per_device(log_beta, gamma_init, topic_prior, word_block, word_row, counts):
    doc_rows, length = counts.shape
    vocab, topic_cols = log_beta.shape
    owners = lax.axis_size("docs")
    tokens = doc_rows * length
    capacity = 2 * tokens // owners
    slots = owners * capacity
    all_docs = owners * doc_rows

    holder = lax.broadcasted_iota(jnp.int32, (doc_rows, length), 0)
    span = doc_rows * vocab * 4
    owner = jnp.where(counts > 0, word_block[:, :, 0], owners)
    packed = owner * span + (holder * vocab + word_row) * 4 + counts
    packed = packed.reshape(tokens)
    edges = jnp.sum(
        packed[None, :] < (jnp.arange(owners + 1, dtype=jnp.int32) * span)[:, None],
        axis=1,
        dtype=jnp.int32,
    )
    ordered = jnp.concatenate([lax.sort(packed), jnp.zeros((capacity,), jnp.int32)])
    pieces = jnp.stack(
        [lax.dynamic_slice(ordered, (edges[o],), (capacity,)) for o in range(owners)]
    )
    held = jnp.arange(capacity, dtype=jnp.int32)[None, :] < (edges[1:] - edges[:-1])[:, None]
    first = jnp.arange(owners, dtype=jnp.int32)[:, None] * span
    request = swap(jnp.where(held, pieces - first, -1))

    source = lax.broadcasted_iota(jnp.int32, (owners, capacity), 0)
    bare = request // 4
    key = ((bare % vocab) * all_docs + source * doc_rows + bare // vocab) * 4 + request % 4
    blank = vocab * all_docs * 4
    key = lax.sort(jnp.where(request < 0, blank, key).reshape(slots))
    valid = key < blank
    rows = jnp.minimum(key // (4 * all_docs), vocab - 1)
    docs = (key // 4) % all_docs
    count = jnp.where(valid, key % 4, 0).astype(jnp.float32)

    def below(height):
        limits = jnp.arange(0, vocab + 1, height, dtype=jnp.int32) * (all_docs * 4)
        return jnp.sum(key[None, :] < limits[:, None], axis=1, dtype=jnp.int32)

    chunk_ends = below(vocab // CHUNKS)
    groups = chunk_ends // GROUP
    groups = groups.at[CHUNKS].set((chunk_ends[CHUNKS] + GROUP - 1) // GROUP)
    found = gather_rows(log_beta, rows, groups).astype(jnp.float32)
    shift = lax.pmax(jnp.max(found, axis=1), "topics")
    mass = jnp.exp(found - shift[:, None])

    chosen = docs[:, None] == jnp.arange(all_docs, dtype=jnp.int32)[None, :]
    doc_gamma = gamma_init
    for sweep_index in range(ITERS + 1):
        theta = jnp.exp(lax.digamma(doc_gamma))
        theta_all = swap(jnp.broadcast_to(theta[None], (owners, doc_rows, topic_cols)))
        theta_all = theta_all.reshape(all_docs, topic_cols)
        products = lax.dot_general(
            mass, theta_all, (((1,), (1,)), ((), ())), precision=lax.Precision.HIGH
        )
        norm = lax.psum(jnp.sum(jnp.where(chosen, products, 0.0), axis=1), "topics")
        weight = count / norm
        if sweep_index < ITERS:
            placed = jnp.where(chosen, weight[:, None], 0.0)
            sums = lax.dot_general(
                placed, mass, (((0,), (0,)), ((), ())), precision=lax.Precision.HIGH
            )
            sums = jnp.sum(swap(sums.reshape(owners, doc_rows, topic_cols)), axis=0)
            doc_gamma = topic_prior[None, :] + theta * sums
    height = 512
    sstats = write_stats(rows, docs, weight, below(height), theta_all, mass, vocab, height)
    return (doc_gamma, sstats)


def solution(mesh):
    in_specs = (
        P("docs", "topics"),
        P("docs", "topics"),
        P("topics"),
        P("docs", None, None),
        P("docs", None),
        P("docs", None),
    )
    out_specs = (P("docs", "topics"), P("docs", "topics"))
    return jax.shard_map(
        per_device, mesh=mesh, in_specs=in_specs, out_specs=out_specs, check_vma=False
    )
```
